1024 devices in a mesh: replica: 128 (over z, y, core), tensor: 8 (over x).
Axes of the slice: x: 8, y: 8, z: 8, core: 2. Of those that a mesh axis runs over, the one named last changes fastest.
Arguments:
- base_stream: bfloat16 [512, 8192], P('tensor', 'replica'), may hold values from -6 to 6
- out_weight: bfloat16 [64, 128, 8192], P('tensor', 'replica'), may hold values from -0.5 to 0.5
- queries: bfloat16 [4, 512, 64, 128], P(None, 'replica', 'tensor'), may hold values from -5 to 5
- cache_keys: bfloat16 [512, 8, 1536, 128], P('replica', 'tensor'), may hold values from -5 to 5
- cache_values: bfloat16 [512, 8, 1536, 128], P('replica', 'tensor'), may hold values from -6 to 6
- new_keys: bfloat16 [4, 512, 8, 128], P(None, 'replica', 'tensor'), may hold values from -5 to 5
- new_values: bfloat16 [4, 512, 8, 128], P(None, 'replica', 'tensor'), may hold values from -6 to 6
- lengths: int32 [512], P('replica'), may hold values from 384 to 1536
- finished: int32 [512], replicated, may hold values 0 or 1
- owners: int32 [512, 1], replicated, may hold values from 0 to 127; in each aligned block of 512 rows (0 to 511, 512 to 1023, ...) at most 8 rows name the same one
Outputs:
- updates: bfloat16 [4, 512, 8192], P(None, 'tensor', 'replica')
- trainer_rows: bfloat16 [128, 8, 8192], P('replica', 'tensor')
The draws below stay inside these ranges and needn't reach their ends.
Inputs may be any that keep to these rules, and one draw needn't show every extreme that they name: `owners`: no owner is named by more than 8 rows, and one owner is named by exactly 8.
All inputs are finite; a program needn't handle non-finite values.
Results may differ from the reference program's by a relative error of at most 0.013.
Values may be sent and summed in bfloat16 or wider, within the bound.
A program may use at most 64 MiB of HBM per device.

```python
import math
import jax
import jax.numpy as jnp
import numpy as np
from jax import lax

D = 8192
QH = 64
KVH = 8
HD = 128
ROW_DEV = 4
CTX = 1536
STEPS = 4
ROWS = 512
CAP = 8
N_REPLICA = 128
N_TENSOR = 8


def shared_parts(key):
    base = jax.random.fold_in(key, 1234)
    key_common = jax.random.fold_in(base, 0)
    common = jax.random.normal(key_common, (STEPS, ROWS, KVH, HD), jnp.float32)
    return common


def draw_queries(key, part):
    common = shared_parts(key)
    group_size = QH // KVH
    own_part = jax.random.normal(jax.random.fold_in(key, 21), (STEPS, ROWS, QH, HD), jnp.float32)
    values = jnp.clip(jnp.repeat(common, group_size, axis=2) + 0.6 * own_part, -5.0, 5.0)
    return values.astype(jnp.bfloat16)


def draw_cache_keys(key, part):
    values = jnp.clip(jax.random.normal(jax.random.fold_in(key, 31), (ROWS, KVH, CTX, HD), jnp.float32), -5.0, 5.0)
    return values.astype(jnp.bfloat16)


def draw_new_keys(key, part):
    common = shared_parts(key)
    noise = jax.random.normal(jax.random.fold_in(key, 41), (STEPS, ROWS, KVH, HD), jnp.float32)
    values = jnp.clip(0.4 * common + 0.7 * noise, -5.0, 5.0)
    return values.astype(jnp.bfloat16)


def touch_ends(values, key, least, top_value):
    shape = values.shape
    spot = [jax.random.randint(jax.random.fold_in(key, axis), (), 0, shape[axis]) for axis in range(len(shape))]
    values = values.at[tuple(spot)].set(least)
    longest = shape.index(max(shape))
    spot[longest] = (spot[longest] + 1) % shape[longest]
    return values.at[tuple(spot)].set(top_value)


def levels(rng, extent, pieces, low, top_value):
    level, own = 1.0, jax.random.fold_in(rng, 6)
    for dim, shards_of in pieces:
        heights = jnp.exp(jax.random.uniform(jax.random.fold_in(own, dim), (shards_of,), jnp.float32, low / len(pieces), top_value / len(pieces)))
        level = level * jnp.repeat(heights, extent[dim] // shards_of).reshape([-1 if axis == dim else 1 for axis in range(len(extent))])
    return level


def shared_out(stream_key, own, number, rows, amount, top, most, skew):
    ranking = jax.random.permutation(stream_key, amount)
    heavy_load, ordinary = portions_of(amount, rows * top, most, skew, True), portions_of(amount, rows * top, most, skew, False)
    places = jnp.arange(amount)

    def named(tallies, offset_by):
        used = int((tallies > 0).sum())
        fixed = max(1, used // 4)
        shifted = fixed + (places - fixed + offset_by * (used - fixed)) % max(1, amount - fixed)
        return jnp.zeros((amount,), jnp.int32).at[ranking[jnp.where(places < fixed, places, shifted)]].set(jnp.asarray(tallies, jnp.int32))

    tallies = jnp.where(number % 4 == 0, named(heavy_load, number // 4), named(ordinary, number - number // 4 - 1))
    mixed = jax.random.permutation(jax.random.fold_in(own, 3), amount)
    donor, taker = mixed[0:amount // 2 * 2:2], mixed[1:amount // 2 * 2:2]
    slack = jnp.minimum(tallies[donor] - 1, most - tallies[taker]) // 2
    slack = jnp.where((donor == ranking[0]) | (taker == ranking[0]) | (tallies[taker] == 0), 0, jnp.maximum(slack, 0))
    shifted = jax.random.randint(jax.random.fold_in(own, 4), (amount // 2,), 0, 1 << 20) % (slack + 1)
    tallies = tallies.at[donor].add(-shifted).at[taker].add(shifted)
    members = jnp.searchsorted(jnp.cumsum(tallies), jnp.arange(rows * top), side="right").astype(jnp.int32)
    listing = members.reshape(top, rows).T
    listing = listing[jax.random.permutation(jax.random.fold_in(own, 1), rows)]
    offset_by = jax.random.randint(jax.random.fold_in(own, 2), (rows, 1), 0, top)
    return jnp.take_along_axis(listing, (jnp.arange(top)[None, :] + offset_by) % top, axis=1)


def portions_of(number_of, total, reach, lean, full):
    portions = [(1 << 20) // math.isqrt(grade ** lean) + 1 for grade in range(1, number_of + 1)]
    largest = reach if full else min(reach, max(-(-total // number_of), total * portions[0] // sum(portions)))
    least = 1 if total - largest >= number_of - 1 else 0
    holding, rest = [largest] + [least] * (number_of - 1), total - largest - least * (number_of - 1)
    while rest > 0:
        movable = [i for i in range(1, number_of) if holding[i] < largest] or [i for i in range(1, number_of) if holding[i] < reach]
        whole, budget = sum([portions[i] for i in movable]), rest
        for i in movable:
            addition = min(reach - holding[i], max(1, budget * portions[i] // whole), rest)
            holding[i] = holding[i] + addition
            rest = rest - addition
    return np.array(holding)


def normal_values(own_key, extent, deviation, limit, pieces=(), kind=jnp.bfloat16):
    result = deviation * jax.random.normal(own_key, extent, jnp.float32)
    if pieces:
        result = result * levels(own_key, extent, pieces, -0.22, 0.18)
    return jnp.clip(result, -limit, limit).astype(kind)


def setup_inputs(seed: int = 0) -> dict:
    splits = jax.random.split(jax.random.key(seed), 11)
    base_stream = normal_values(splits[0], (ROWS, D), 1.0, 6.0, ((0, 8), (1, 128)))
    out_weight = normal_values(splits[1], (QH, HD, D), HD ** -0.5, 0.5, ((0, 8), (1, 128)))
    queries = draw_queries(jax.random.fold_in(splits[10], 71), 0)
    cache_keys = draw_cache_keys(jax.random.fold_in(splits[10], 71), 0)
    cache_values = normal_values(splits[4], (ROWS, KVH, CTX, HD), 1.0, 6.0, ((0, 128), (1, 8)))
    new_keys = draw_new_keys(jax.random.fold_in(splits[10], 71), 0)
    new_values = normal_values(splits[6], (STEPS, ROWS, KVH, HD), 1.0, 6.0, ((1, 128), (2, 8)))
    lengths = touch_ends(jax.random.randint(splits[7], (ROWS,), CTX // 4, CTX + 1), jax.random.fold_in(splits[7], 1), CTX // 4, CTX).astype(jnp.int32)
    finished = touch_ends((jax.random.randint(splits[8], (ROWS,), 0, 4) < 3).astype(jnp.int32), jax.random.fold_in(splits[8], 1), 0, 1)
    owners_keys = jax.random.split(jax.random.fold_in(splits[9], 1), ROWS // ROWS)
    owners_turns = jax.random.permutation(jax.random.fold_in(splits[9], 3), ROWS // ROWS)
    owners = jax.vmap(lambda own, number: shared_out(jax.random.fold_in(splits[9], 2), own, number, ROWS, N_REPLICA, 1, CAP, 2))(owners_keys, owners_turns).reshape((ROWS, 1))
    return dict(base_stream=base_stream, out_weight=out_weight, queries=queries, cache_keys=cache_keys, cache_values=cache_values, new_keys=new_keys, new_values=new_values, lengths=lengths, finished=finished, owners=owners)


def attend_block(block):
    query_rows, key_rows, value_rows, fresh_keys, fresh_values, row_lengths = block
    group_size = QH // KVH
    count = query_rows.shape[1]
    score_scale = 1.0 / math.sqrt(HD)
    grouped = query_rows.astype(jnp.float32).reshape(STEPS, count, KVH, group_size, HD)
    cache_scores = jnp.einsum('tbgqd,bgcd->tbgqc', grouped, key_rows.astype(jnp.float32)) * score_scale
    positions = lax.broadcasted_iota(jnp.int32, (1, count, 1, 1, CTX), 4)
    is_valid = positions < row_lengths.astype(jnp.int32)[None, :, None, None, None]
    cache_scores = jnp.where(is_valid, cache_scores, jnp.float32(-1e+30))
    fresh_scores = jnp.einsum('tbgqd,ubgd->tbgqu', grouped, fresh_keys.astype(jnp.float32)) * score_scale
    step_now = lax.broadcasted_iota(jnp.int32, (STEPS, 1, 1, 1, STEPS), 0)
    step_then = lax.broadcasted_iota(jnp.int32, (STEPS, 1, 1, 1, STEPS), 4)
    fresh_scores = jnp.where(step_then <= step_now, fresh_scores, jnp.float32(-1e+30))
    highest = jnp.maximum(lax.optimization_barrier(jnp.max(cache_scores, axis=-1, keepdims=True)), lax.optimization_barrier(jnp.max(fresh_scores, axis=-1, keepdims=True)))
    cache_weights = jnp.exp(cache_scores - highest)
    fresh_weights = jnp.exp(fresh_scores - highest)
    totals = lax.optimization_barrier(jnp.sum(cache_weights, axis=-1, keepdims=True)) + lax.optimization_barrier(jnp.sum(fresh_weights, axis=-1, keepdims=True))
    cache_probs = (cache_weights / totals).astype(jnp.bfloat16).astype(jnp.float32)
    fresh_probs = (fresh_weights / totals).astype(jnp.bfloat16).astype(jnp.float32)
    mixed = jnp.einsum('tbgqc,bgcd->tbgqd', cache_probs, value_rows.astype(jnp.float32))
    mixed = mixed + jnp.einsum('tbgqu,ubgd->tbgqd', fresh_probs, fresh_values.astype(jnp.float32))
    return mixed.reshape(STEPS, count, QH * HD).astype(jnp.bfloat16)

def reference(base_stream, out_weight, queries, cache_keys, cache_values, new_keys, new_values, lengths, finished, owners):
    block_rows = ROW_DEV
    blocks = ROWS // block_rows
    query_blocks = queries.reshape(STEPS, blocks, block_rows, QH, HD).transpose(1, 0, 2, 3, 4)
    key_blocks = cache_keys.reshape(blocks, block_rows, KVH, CTX, HD)
    value_blocks = cache_values.reshape(blocks, block_rows, KVH, CTX, HD)
    fresh_key_blocks = new_keys.reshape(STEPS, blocks, block_rows, KVH, HD).transpose(1, 0, 2, 3, 4)
    fresh_value_blocks = new_values.reshape(STEPS, blocks, block_rows, KVH, HD).transpose(1, 0, 2, 3, 4)
    length_blocks = lengths.reshape(blocks, block_rows)
    attended = lax.map(attend_block, (query_blocks, key_blocks, value_blocks, fresh_key_blocks, fresh_value_blocks, length_blocks))
    attended = attended.transpose(1, 0, 2, 3).reshape(STEPS * ROWS, QH * HD)
    weight_flat = out_weight.reshape(QH * HD, D)
    group_width = QH // N_TENSOR * HD
    projected = jnp.zeros((STEPS * ROWS, D), jnp.float32)
    for group in range(N_TENSOR):
        lower = group * group_width
        upper = lower + group_width
        partial_value = jnp.dot(attended[:, lower:upper], weight_flat[lower:upper], preferred_element_type=jnp.float32)
        rounded = lax.optimization_barrier(partial_value.astype(jnp.bfloat16))
        projected = projected + rounded.astype(jnp.float32)
    updates = projected.reshape(STEPS, ROWS, D).astype(jnp.bfloat16)
    stream = base_stream.astype(jnp.float32) + lax.optimization_barrier(jnp.sum(updates.astype(jnp.float32), axis=0))
    owner_ids = lax.broadcasted_iota(jnp.int32, (1, N_REPLICA), 1)
    onehot = (owners.astype(jnp.int32) == owner_ids).astype(jnp.int32)
    running = jnp.cumsum(onehot, axis=0)
    slot_rank = lax.optimization_barrier(jnp.sum((running - onehot) * onehot, axis=1)).astype(jnp.int32)
    slot_index = (owners[:, 0].astype(jnp.int32) * CAP + slot_rank).astype(jnp.int32)
    handed = stream.astype(jnp.bfloat16) * finished.astype(jnp.bfloat16)[:, None]
    buffer = jnp.zeros((N_REPLICA * CAP, D), jnp.bfloat16).at[slot_index].set(handed)
    trainer_rows = buffer.reshape(N_REPLICA, CAP, D)
    return (updates, trainer_rows)
```

```python
import functools
import math

import jax
import jax.numpy as jnp
from jax import lax
from jax.experimental import pallas as pl
from jax.experimental.pallas import tpu as pltpu
from jax.sharding import Mesh
from jax.sharding import PartitionSpec as P

ZA, YA, CA, XA = "replica_0", "replica_1", "replica_2", "tensor"
REPLICA = (ZA, YA, CA)
MESH = pl.DeviceIdType.MESH
F32, BF16, I32 = jnp.float32, jnp.bfloat16, jnp.int32
N = 8
CTX = 1536
PAD = 128
FULL = CTX + PAD
ROWS = 512


def dot(a, b):
    return jnp.dot(a, b, preferred_element_type=F32)


def iota(shape, dim):
    return lax.broadcasted_iota(I32, shape, dim)


def offset_of(j):
    return (j + 1) // 2 * (2 * (j % 2) - 1)


def mirror(j):
    if j == 0 or j == N - 1:
        return j
    return j + 1 if j % 2 else j - 1


def kernel(
    len_ref, q_hbm, k_hbm, v_hbm, nk_hbm, nv_hbm, w_hbm, base_hbm, own_hbm, fin_hbm,
    upd_hbm, tr_hbm,
    q_v, k_v, v_v, nk_v, nv_v, base_v, own_v, fin_v,
    s1, wbuf, wf, w4, att, g0, g1, cs, cr, sp, sg, sgu, oh, o1, r1, tf, t2, r2, uout, trout,
    in_sem, kv_sem, out_sem,
    w_send, w1_recv, w2_recv, w3_recv,
    p_send, p_recv, ring_send, ring_recv,
    c_send, c_recv, s_send, s_recv, z_send, z_recv, y_send, y_recv,
):
    z, y, c, x = (lax.axis_index(a) for a in (ZA, YA, CA, XA))
    other = 1 - c

    def rot(i, d):
        return lax.rem(i + d + N, N)

    def remote(src, dst, ssem, rsem, **to):
        pltpu.make_async_remote_copy(
            src_ref=src, dst_ref=dst, send_sem=ssem, recv_sem=rsem,
            device_id={{"z": ZA, "y": YA, "c": CA, "x": XA}[k]: v for k, v in to.items()},
            device_id_type=MESH,
        ).start()

    def arrived(ref, sem):
        pltpu.make_async_copy(ref, ref, sem).wait()

    small = [
        (q_hbm, q_v), (nk_hbm, nk_v), (nv_hbm, nv_v), (base_hbm, base_v), (own_hbm, own_v), (fin_hbm, fin_v),
    ]
    loads = [pltpu.make_async_copy(a, b, in_sem.at[i]) for i, (a, b) in enumerate(small)]
    k_loads = [pltpu.make_async_copy(k_hbm.at[b], k_v.at[b, pl.ds(0, CTX)], kv_sem.at[0, b]) for b in range(4)]
    v_loads = [pltpu.make_async_copy(v_hbm.at[b], v_v.at[b, pl.ds(0, CTX)], kv_sem.at[1, b]) for b in range(4)]
    for load in loads[:3]:
        load.start()
    for b in range(4):
        k_loads[b].start()
        v_loads[b].start()
    for load in loads[3:]:
        load.start()

    barrier = pltpu.get_barrier_semaphore()

    def greet(**to):
        pl.semaphore_signal(
            barrier, inc=1, device_id={{"z": ZA, "y": YA, "c": CA, "x": XA}[k]: v for k, v in to.items()},
            device_id_type=MESH,
        )

    greet(c=other)

    def greet_step(d, carry):
        greet(z=rot(z, d))
        greet(y=rot(y, d), c=0)
        greet(y=rot(y, d), c=1)
        greet(x=rot(x, d), c=0)
        greet(x=rot(x, d), c=1)
        return carry

    lax.fori_loop(1, N, greet_step, 0)

    for load in loads[:3]:
        load.wait()
    nk, nv = nk_v[...], nv_v[...]
    for b in range(4):
        pick = (iota((PAD, 16), 1) == iota((PAD, 16), 0) * 4 + b).astype(F32).astype(BF16)
        k_v[b, CTX:FULL, :] = dot(pick, nk).astype(BF16)
        v_v[b, CTX:FULL, :] = dot(pick, nv).astype(BF16)

    scale = 1.0 / math.sqrt(128.0)

    def attend(b):
        q = q_v[:, b].astype(F32).reshape(32, 128).astype(BF16)
        k_loads[b].wait()
        scores = lax.dot_general(q, k_v[b], (((1,), (1,)), ((), ())), preferred_element_type=F32) * scale
        col = iota((32, FULL), 1)
        step = iota((32, FULL), 0) // 8
        keep = (col < len_ref[b]) | ((col >= CTX) & (col - CTX <= step))
        scores = jnp.where(keep, scores, F32(-1e30))
        high = jnp.max(scores, axis=-1, keepdims=True)
        weight = jnp.exp(scores - high)
        total = jnp.sum(weight, axis=-1, keepdims=True)
        probs = (weight / total).astype(BF16)
        v_loads[b].wait()
        mixed = dot(probs, v_v[b])
        for t in range(4):
            att[pl.ds((t * 4 + b) * 8, 8), :] = mixed[t * 8 : t * 8 + 8]

    attend(0)
    attend(1)
    pl.semaphore_wait(barrier, 5 * (N - 1) + 1)

    own_w = pltpu.make_async_copy(w_hbm.at[:, pl.ds(pl.multiple_of(z * 1024, 1024), 1024)], s1.at[z], in_sem.at[6])
    own_w.start()

    def w1_step(d, carry):
        zt = rot(z, d)
        remote(w_hbm.at[:, pl.ds(pl.multiple_of(zt * 1024, 1024), 1024)], s1.at[z], w_send.at[0], w1_recv.at[d], z=zt)
        return carry

    lax.fori_loop(1, N, w1_step, 0)
    attend(2)
    attend(3)
    for h in range(8):
        part = att[pl.ds(h, 16, stride=8), :].astype(BF16)
        (g0 if h < 4 else g1)[z, y, :, (h % 4) * 128 : (h % 4) * 128 + 128] = part

    for j in range(1, N):
        o = offset_of(j)
        remote(g0.at[z, y], g0.at[z, y], p_send.at[0], p_recv.at[0, mirror(j)], y=rot(y, o))
        remote(g1.at[z, y], g1.at[z, y], p_send.at[1], p_recv.at[1, mirror(j)], z=rot(z, o))

    def unit(stream, s, j):
        o = offset_of(j)
        if stream == 0:
            return g0.at[rot(z, -s), rot(y, o)]
        if stream == 1:
            return g0.at[rot(z, s), rot(y, o)]
        if stream == 2:
            return g1.at[rot(z, o), rot(y, -s)]
        return g1.at[rot(z, o), rot(y, s)]

    def forward(stream, s, j):
        to = ({"z": rot(z, 1)}, {"z": rot(z, -1)}, {"y": rot(y, 1)}, {"y": rot(y, -1)})[stream]
        block = unit(stream, s, j)
        remote(block, block, ring_send.at[stream], ring_recv.at[stream, s * N + j], **to)

    def came(stream, s, j):
        arrived(unit(stream, s + 1, j), ring_recv.at[stream, s * N + j])

    for stream in range(4):
        forward(stream, 0, 0)

    def level0(j, carry):
        o = offset_of(j)
        arrived(g0.at[z, rot(y, o)], p_recv.at[0, j])
        forward(0, 0, j)
        forward(1, 0, j)
        arrived(g1.at[rot(z, o), y], p_recv.at[1, j])
        forward(2, 0, j)
        forward(3, 0, j)
        return carry

    lax.fori_loop(1, N, level0, 0)

    def w1_wait(d, carry):
        zs = rot(z, -d)
        arrived(s1.at[zs], w1_recv.at[d])
        return carry

    own_w.wait()
    lax.fori_loop(1, N, w1_wait, 0)

    def w2_step(d, carry):
        yt = rot(y, d)
        remote(
            s1.at[:, :, pl.ds(pl.multiple_of(yt * 128, 128), 128)], wbuf.at[:, y, c], w_send.at[1], w2_recv.at[d], y=yt
        )
        return carry

    lax.fori_loop(1, N, w2_step, 0)
    own_w2 = pltpu.make_async_copy(
        s1.at[:, :, pl.ds(pl.multiple_of(y * 128, 128), 128)], wbuf.at[:, y, c], in_sem.at[7]
    )
    own_w2.start()

    def ring_step(k, carry):
        s, j = k // N, k % N
        for stream in range(4):
            came(stream, s - 1, j)
            forward(stream, s, j)
        return carry

    lax.fori_loop(N, 2 * N, ring_step, 0)

    def w2_wait(d, carry):
        arrived(wbuf.at[:, rot(y, -d), c], w2_recv.at[d])
        return carry

    own_w2.wait()
    lax.fori_loop(1, N, w2_wait, 0)
    remote(wbuf.at[:, :, c], wbuf.at[:, :, c], w_send.at[2], w3_recv, c=other)

    lax.fori_loop(2 * N, 3 * N, ring_step, 0)

    def last_step(j, carry):
        for stream in (0, 2):
            came(stream, 2, j)
            forward(stream, 3, j)
        for stream in (1, 3):
            came(stream, 2, j + 4)
            forward(stream, 3, j + 4)
        return carry

    lax.fori_loop(0, N // 2, last_step, 0)

    arrived(wbuf.at[:, :, other], w3_recv)
    wf[...] = wbuf[...].astype(F32).reshape(1024, 128)
    left = iota((128, 128), 1) < 64
    for h in range(8):
        part = wf[pl.ds(h, 128, stride=8), :]
        turned = pltpu.roll(part, 64, 1)
        w4[h * 128 : h * 128 + 128, 0:128] = jnp.where(left, part, turned).astype(BF16)
        w4[h * 128 : h * 128 + 128, 128:256] = jnp.where(left, turned, part).astype(BF16)

    def last_wait(j, carry):
        for stream in (0, 2):
            came(stream, 2, j + 4)
            came(stream, 3, j)
        for stream in (1, 3):
            came(stream, 2, j)
            came(stream, 3, j + 4)
        return carry

    lax.fori_loop(0, N // 2, last_wait, 0)

    half = iota((64, 128), 1) < 64
    for d in (4, 3, 5, 2, 6, 1, 7, 0):
        xt = rot(x, d)
        part = dot(g0[xt].reshape(128, 512), w4[0:512]) + dot(g1[xt].reshape(128, 512), w4[512:1024])
        top, bottom = part[0:64], part[64:128]
        to0 = jnp.where(half, top[:, 0:128], bottom[:, 0:128]).astype(BF16)
        to1 = jnp.where(half, top[:, 128:256], bottom[:, 128:256]).astype(BF16)
        cs[0, xt] = to0
        cs[1, xt] = to1
        if d:
            remote(cs.at[0, xt], cr.at[x * 2 + c], c_send, c_recv.at[2 * d + c], x=xt, c=0)
            remote(cs.at[1, xt], cr.at[x * 2 + c], c_send, c_recv.at[2 * d + c], x=xt, c=1)
        else:
            remote(cs.at[other, x], cr.at[x * 2 + c], c_send, c_recv.at[c], c=other)
            cr[x * 2 + c] = cs[c, x]

    loads[3].wait()
    loads[4].wait()
    loads[5].wait()
    row = iota((128, ROWS), 0)
    owner = (row % 64) * 2 + row // 64
    mine = (own_v[...] == owner).astype(F32)
    earlier = (iota((ROWS, ROWS), 0) < iota((ROWS, ROWS), 1)).astype(F32).astype(BF16)
    before = dot(mine.astype(BF16), earlier)
    slot = jnp.where(before == x.astype(F32), mine, F32(0)) * fin_v[...].astype(F32)
    oh[...] = slot.astype(BF16)
    base = base_v[...].astype(F32)
    base = jnp.concatenate([base[0:32], base[32:64]], axis=1)
    a, b = iota((128, 128), 0), iota((128, 128), 1)
    source = (a // 4 % 2) * 64 + (a // 8 % 4) * 16 + (a // 32) * 4 + a % 4
    order = (b == source).astype(F32).astype(BF16)

    def c_wait(d, carry):
        arrived(cr.at[rot(x, -d) * 2], c_recv.at[2 * d])
        arrived(cr.at[rot(x, -d) * 2 + 1], c_recv.at[2 * d + 1])
        return carry

    arrived(cr.at[x * 2 + other], c_recv.at[other])
    lax.fori_loop(1, N, c_wait, 0)
    summed = cr[pl.ds(0, 2)].astype(F32)
    for i in range(1, N):
        summed = summed + cr[pl.ds(2 * i, 2)].astype(F32)
    rows = dot(order, summed.reshape(128, 128).astype(BF16))
    stream = base + (((rows[0:32] + rows[32:64]) + rows[64:96]) + rows[96:128])
    sp[...] = stream.astype(BF16)

    def s_step(d, carry):
        remote(sp, sg.at[x], s_send, s_recv.at[d], x=rot(x, d))
        return carry

    lax.fori_loop(1, N, s_step, 0)
    sg[x] = sp[...]
    turned = pltpu.roll(rows, 64, 1)
    for t in range(4):
        uout[t, 0:32, :] = rows[t * 32 : t * 32 + 32, 0:64].astype(BF16)
        uout[t, 32:64, :] = turned[t * 32 : t * 32 + 32, 0:64].astype(BF16)
    save_updates = pltpu.make_async_copy(uout, upd_hbm, out_sem.at[0])
    save_updates.start()

    def s_wait(d, carry):
        arrived(sg.at[rot(x, -d)], s_recv.at[d])
        return carry

    lax.fori_loop(1, N, s_wait, 0)

    for i in range(N):
        block = sg[i].astype(F32)
        sgu[i * 64 : i * 64 + 32, :] = block.astype(BF16)
        sgu[i * 64 + 32 : i * 64 + 64, :] = pltpu.roll(block, 64, 1).astype(BF16)
    chosen = dot(oh[...], sgu[...])
    packed = jnp.where(half, chosen[0:64], pltpu.roll(chosen[64:128], 64, 1))
    o1[...] = packed.reshape(8, 8, 128).astype(BF16)

    def z_step(d, carry):
        zt = rot(z, d)
        remote(o1.at[zt], r1.at[z], z_send, z_recv.at[d], z=zt)
        return carry

    lax.fori_loop(1, N, z_step, 0)
    r1[z] = o1[z]

    def z_wait(d, carry):
        arrived(r1.at[rot(z, -d)], z_recv.at[d])
        return carry

    lax.fori_loop(1, N, z_wait, 0)
    tf[...] = r1[...].astype(F32).reshape(64, 128)
    for i in range(N):
        t2[i] = tf[pl.ds(i, 8, stride=8), :].astype(BF16)

    def y_step(d, carry):
        yt = rot(y, d)
        remote(t2.at[yt], r2.at[y * 2 + c], y_send, y_recv.at[2 * d + c], y=yt, c=0)
        remote(t2.at[yt], r2.at[y * 2 + c], y_send, y_recv.at[2 * d + c], y=yt, c=1)
        return carry

    remote(t2.at[y], r2.at[y * 2 + c], y_send, y_recv.at[c], c=other)
    lax.fori_loop(1, N, y_step, 0)
    r2[y * 2 + c] = t2[y]

    def y_wait(d, carry):
        arrived(r2.at[rot(y, -d) * 2], y_recv.at[2 * d])
        arrived(r2.at[rot(y, -d) * 2 + 1], y_recv.at[2 * d + 1])
        return carry

    arrived(r2.at[y * 2 + other], y_recv.at[other])
    lax.fori_loop(1, N, y_wait, 0)
    eighth = iota((8, 128), 1) < 64
    for i in range(N):
        v0, v1 = r2[2 * i].astype(F32), r2[2 * i + 1].astype(F32)
        a0 = jnp.where(c == 0, v0, pltpu.roll(v0, 64, 1))
        a1 = jnp.where(c == 0, pltpu.roll(v1, 64, 1), v1)
        tf[i * 8 : i * 8 + 8, :] = jnp.where(eighth, a0, a1)
    for i in range(N):
        trout[i * 8 : i * 8 + 8, :] = tf[pl.ds(i, 8, stride=8), :].astype(BF16)
    save_rows = pltpu.make_async_copy(trout, tr_hbm, out_sem.at[1])
    save_rows.start()

    arrived(s1.at[pl.ds(0, 7)], w_send.at[0])
    arrived(s1.at[pl.ds(0, 7)], w_send.at[1])
    arrived(wbuf.at[:, :, c], w_send.at[2])
    arrived(g0.at[0, pl.ds(0, 7)], p_send.at[0])
    arrived(g0.at[0, pl.ds(0, 7)], p_send.at[1])
    for i in range(4):
        arrived(g0.at[pl.ds(0, 7), pl.ds(0, 4)], ring_send.at[i])
    arrived(cr.at[pl.ds(0, 15)], c_send)
    arrived(sg.at[pl.ds(0, 7)], s_send)
    arrived(r1.at[pl.ds(0, 7)], z_send)
    arrived(r2.at[pl.ds(0, 15)], y_send)
    save_updates.wait()
    save_rows.wait()


def shards(base_stream, out_weight, queries, cache_keys, cache_values, new_keys, new_values, lengths, finished, owners):
    hbm = pl.BlockSpec(memory_space=pl.ANY)
    dma = pltpu.SemaphoreType.DMA
    updates, rows = pl.pallas_call(
        kernel,
        out_shape=(jax.ShapeDtypeStruct((4, 64, 64), BF16), jax.ShapeDtypeStruct((64, 128), BF16)),
        in_specs=[pl.BlockSpec(memory_space=pltpu.SMEM)] + [hbm] * 9,
        out_specs=(hbm, hbm),
        scratch_shapes=[
            pltpu.VMEM((4, 4, 8, 128), BF16),
            pltpu.VMEM((4, FULL, 128), BF16),
            pltpu.VMEM((4, FULL, 128), BF16),
            pltpu.VMEM((16, 128), BF16),
            pltpu.VMEM((16, 128), BF16),
            pltpu.VMEM((64, 64), BF16),
            pltpu.VMEM((1, ROWS), I32),
            pltpu.VMEM((1, ROWS), I32),
            pltpu.VMEM((8, 8, 1024), BF16),
            pltpu.VMEM((8, 8, 2, 8, 128), BF16),
            pltpu.VMEM((1024, 128), F32),
            pltpu.VMEM((1024, 256), BF16),
            pltpu.VMEM((128, 128), F32),
            pltpu.VMEM((8, 8, 16, 512), BF16),
            pltpu.VMEM((8, 8, 16, 512), BF16),
            pltpu.VMEM((2, 8, 64, 128), BF16),
            pltpu.VMEM((16, 64, 128), BF16),
            pltpu.VMEM((32, 128), BF16),
            pltpu.VMEM((8, 32, 128), BF16),
            pltpu.VMEM((ROWS, 128), BF16),
            pltpu.VMEM((128, ROWS), BF16),
            pltpu.VMEM((8, 8, 128), BF16),
            pltpu.VMEM((8, 8, 128), BF16),
            pltpu.VMEM((64, 128), F32),
            pltpu.VMEM((8, 8, 128), BF16),
            pltpu.VMEM((16, 8, 128), BF16),
            pltpu.VMEM((4, 64, 64), BF16),
            pltpu.VMEM((64, 128), BF16),
            dma((8,)),
            dma((2, 4)),
            dma((2,)),
            dma((3,)),
            dma((8,)),
            dma((8,)),
            dma,
            dma((2,)),
            dma((2, 8)),
            dma((4,)),
            dma((4, 32)),
            dma,
            dma((16,)),
            dma,
            dma((8,)),
            dma,
            dma((8,)),
            dma,
            dma((16,)),
        ],
        compiler_params=pltpu.CompilerParams(collective_id=0, has_side_effects=True),
        name="decode",
    )(
        lengths,
        queries,
        cache_keys.reshape(4, CTX, 128),
        cache_values.reshape(4, CTX, 128),
        new_keys.reshape(16, 128),
        new_values.reshape(16, 128),
        out_weight.reshape(8, 8192),
        base_stream,
        owners.reshape(1, ROWS),
        finished.reshape(1, ROWS),
    )
    return updates, rows.reshape(1, 1, 8192)


def solution(mesh):
    torus = Mesh(mesh.devices.reshape(N, N, 2, N), (ZA, YA, CA, XA))
    placed = (
        P(XA, REPLICA),
        P(XA, REPLICA, None),
        P(None, REPLICA, XA, None),
        P(REPLICA, XA, None, None),
        P(REPLICA, XA, None, None),
        P(None, REPLICA, XA, None),
        P(None, REPLICA, XA, None),
        P(REPLICA),
        P(),
        P(),
    )
    return jax.shard_map(
        shards, mesh=torus, in_specs=placed, out_specs=(P(None, XA, REPLICA), P(REPLICA, XA, None)), check_vma=False
    )
```

```python
import functools
import math

import jax
import jax.numpy as jnp
from jax import lax
from jax.experimental import pallas as pl
from jax.experimental.pallas import tpu as pltpu
from jax.sharding import Mesh
from jax.sharding import PartitionSpec as P

ZA, YA, CA, XA = "replica_0", "replica_1", "replica_2", "tensor"
REPLICA = (ZA, YA, CA)
MESH = pl.DeviceIdType.MESH
F32, BF16, I32 = jnp.float32, jnp.bfloat16, jnp.int32
N = 8
CTX = 1536
PAD = 128
FULL = CTX + PAD
ROWS = 512


def dot(a, b):
    return jnp.dot(a, b, preferred_element_type=F32)


def iota(shape, dim):
    return lax.broadcasted_iota(I32, shape, dim)


def offset_of(j):
    return (j + 1) // 2 * (2 * (j % 2) - 1)


def mirror(j):
    if j == 0 or j == N - 1:
        return j
    return j + 1 if j % 2 else j - 1


def kernel(
    len_hbm, q_hbm, k_hbm, v_hbm, nk_hbm, nv_hbm, w_hbm, base_hbm, own_hbm, fin_hbm,
    rows_out, r2,
    len_s, q_v, k_v, v_v, nk_v, nv_v, base_v, own_v, fin_v,
    sa, sb, wbuf, wf, w4, att, g0, g1, part0, part1, pn, ts, tr, cs, cr, bp, bg, sgu, oh, o1, r1, tf, t2,
    in_sem, kv_sem,
    w_send, w1_recv, w2_recv, w3_recv,
    p_send, p_recv, ring_send, ring_recv,
    t_send, t_recv, c_send, c_recv, b_send, b_recv, z_send, z_recv, y_send, y_recv,
):
    z, y, c, x = (lax.axis_index(a) for a in (ZA, YA, CA, XA))
    other = 1 - c

    def rot(i, d):
        return lax.rem(i + d + N, N)

    def remote(src, dst, ssem, rsem, **to):
        pltpu.make_async_remote_copy(
            src_ref=src, dst_ref=dst, send_sem=ssem, recv_sem=rsem,
            device_id={{"z": ZA, "y": YA, "c": CA, "x": XA}[k]: v for k, v in to.items()},
            device_id_type=MESH,
        ).start()

    def arrived(ref, sem):
        pltpu.make_async_copy(ref, ref, sem).wait()

    small = [
        (q_hbm, q_v), (nk_hbm, nk_v), (nv_hbm, nv_v), (len_hbm, len_s),
        (base_hbm, base_v), (own_hbm, own_v), (fin_hbm, fin_v),
    ]
    loads = [pltpu.make_async_copy(a, b, in_sem.at[i]) for i, (a, b) in enumerate(small)]
    k_loads = [pltpu.make_async_copy(k_hbm.at[b], k_v.at[b, pl.ds(0, CTX)], kv_sem.at[0, b]) for b in range(4)]
    v_loads = [pltpu.make_async_copy(v_hbm.at[b], v_v.at[b, pl.ds(0, CTX)], kv_sem.at[1, b]) for b in range(4)]
    for load in loads[:4]:
        load.start()
    for b in range(4):
        k_loads[b].start()
        v_loads[b].start()
    for load in loads[4:]:
        load.start()

    barrier = pltpu.get_barrier_semaphore()

    def greet(**to):
        pl.semaphore_signal(
            barrier, inc=1, device_id={{"z": ZA, "y": YA, "c": CA, "x": XA}[k]: v for k, v in to.items()},
            device_id_type=MESH,
        )

    greet(c=other)

    def greet_step(d, carry):
        greet(z=rot(z, d))
        greet(y=rot(y, d), c=0)
        greet(y=rot(y, d), c=1)
        greet(x=rot(x, d), c=0)
        greet(x=rot(x, d), c=1)
        return carry

    lax.fori_loop(1, N, greet_step, 0)

    for load in loads[:4]:
        load.wait()
    nk, nv = nk_v[...], nv_v[...]
    for b in range(4):
        pick = (iota((PAD, 16), 1) == iota((PAD, 16), 0) * 4 + b).astype(F32).astype(BF16)
        k_v[b, CTX:FULL, :] = dot(pick, nk).astype(BF16)
        v_v[b, CTX:FULL, :] = dot(pick, nv).astype(BF16)

    scale = 1.0 / math.sqrt(128.0)

    def attend(b):
        q = q_v[:, b].astype(F32).reshape(32, 128).astype(BF16)
        k_loads[b].wait()
        scores = lax.dot_general(q, k_v[b], (((1,), (1,)), ((), ())), preferred_element_type=F32) * scale
        col = iota((32, FULL), 1)
        step = iota((32, FULL), 0) // 8
        keep = (col < len_s[b]) | ((col >= CTX) & (col - CTX <= step))
        scores = jnp.where(keep, scores, F32(-1e30))
        high = jnp.max(scores, axis=-1, keepdims=True)
        weight = jnp.exp(scores - high)
        total = jnp.sum(weight, axis=-1, keepdims=True)
        probs = (weight / total).astype(BF16)
        v_loads[b].wait()
        mixed = dot(probs, v_v[b])
        for t in range(4):
            att[pl.ds((t * 4 + b) * 8, 8), :] = mixed[t * 8 : t * 8 + 8]

    attend(0)
    attend(1)
    attend(2)
    pl.semaphore_wait(barrier, 5 * (N - 1) + 1)

    def via_z(zt):
        return w_hbm.at[zt // 2, zt % 2, :, zt % 2]

    def via_y(yt):
        return w_hbm.at[:, (yt + 1) % 2, yt // 2, yt % 2]

    own_w = [
        pltpu.make_async_copy(via_z(z), sa.at[z], in_sem.at[7]),
        pltpu.make_async_copy(via_y(y), sb.at[y], in_sem.at[8]),
    ]
    for load in own_w:
        load.start()

    def w1_step(d, carry):
        zt, yt = rot(z, d), rot(y, d)
        remote(via_z(zt), sa.at[z], w_send.at[0], w1_recv, z=zt)
        remote(via_y(yt), sb.at[y], w_send.at[0], w1_recv, y=yt)
        return carry

    lax.fori_loop(1, N, w1_step, 0)

    for load in loads[4:]:
        load.wait()
    base = base_v[...].astype(F32)
    bp[...] = jnp.concatenate([base[0:32], base[32:64]], axis=1).astype(BF16)

    def base_step(d, carry):
        remote(bp, bg.at[x], b_send, b_recv, x=rot(x, d))
        return carry

    lax.fori_loop(1, N, base_step, 0)
    bg[x] = bp[...]
    attend(3)
    for h in range(8):
        part = att[pl.ds(h, 16, stride=8), :].astype(BF16)
        (g0 if h < 4 else g1)[z, y, :, (h % 4) * 128 : (h % 4) * 128 + 128] = part

    for j in range(1, N):
        o = offset_of(j)
        remote(g0.at[z, y], g0.at[z, y], p_send.at[0], p_recv.at[0, mirror(j) // 2], y=rot(y, o))
        remote(g1.at[z, y], g1.at[z, y], p_send.at[1], p_recv.at[1, mirror(j) // 2], z=rot(z, o))

    def unit(stream, s, j):
        o = offset_of(j)
        if stream == 0:
            return g0.at[rot(z, -s), rot(y, o)]
        if stream == 1:
            return g0.at[rot(z, s), rot(y, o)]
        if stream == 2:
            return g1.at[rot(z, o), rot(y, -s)]
        return g1.at[rot(z, o), rot(y, s)]

    def slot_of(s, pair):
        return s * 4 + (pair % 2 if isinstance(s, int) and s == 3 else pair)

    def forward(stream, s, pair, places=(0, 1)):
        to = ({"z": rot(z, 1)}, {"z": rot(z, -1)}, {"y": rot(y, 1)}, {"y": rot(y, -1)})[stream]
        for i in places:
            block = unit(stream, s, pair * 2 + i)
            remote(block, block, ring_send.at[stream], ring_recv.at[stream, slot_of(s, pair)], **to)

    def came(stream, s, pair):
        arrived(g0.at[0, pl.ds(0, 2)], ring_recv.at[stream, slot_of(s, pair)])

    for stream in range(4):
        forward(stream, 0, 0, (0,))

    def level0(pair):
        for half_of in range(2):
            arrived(g0.at[0, pl.ds(0, 2 if pair else 1)], p_recv.at[half_of, pair])
            for stream in (2 * half_of, 2 * half_of + 1):
                forward(stream, 0, pair, (0, 1) if pair else (1,))

    level0(0)
    level0(1)

    for load in own_w:
        load.wait()
    arrived(g0.at[0, pl.ds(0, 7)], w1_recv)
    even = (z + y) % 2 == 0

    def w2_step(i, carry):
        yt, zt = 2 * i + z % 2, 2 * i + (y + 1) % 2

        @pl.when(yt != y)
        def _():
            remote(sa.at[:, i], wbuf.at[:, y, c], w_send.at[0], w2_recv, y=yt)

        @pl.when(zt != z)
        def _():
            remote(sb.at[:, i], wbuf.at[z, :, c], w_send.at[0], w2_recv, z=zt)

        return carry

    lax.fori_loop(0, N // 2, w2_step, 0)

    @pl.when(even)
    def _():
        pltpu.make_async_copy(sa.at[:, y // 2], wbuf.at[:, y, c], in_sem.at[9]).start()

    @pl.when(jnp.logical_not(even))
    def _():
        pltpu.make_async_copy(sb.at[:, z // 2], wbuf.at[z, :, c], in_sem.at[9]).start()

    level0(2)
    level0(3)

    def ring_step(k, carry):
        s, pair = k // 4, k % 4
        for stream in range(4):
            came(stream, s - 1, pair)
            forward(stream, s, pair)
        return carry

    lax.fori_loop(4, 12, ring_step, 0)

    arrived(g0.at[0, pl.ds(0, 1)], in_sem.at[9])
    arrived(g0.at[0, pl.ds(0, 7)], w2_recv)
    remote(wbuf.at[:, :, c], wbuf.at[:, :, c], w_send.at[1], w3_recv, c=other)

    for pair in range(2):
        for stream in range(4):
            mine_of = pair + 2 * (stream % 2)
            came(stream, 2, mine_of)
            forward(stream, 3, mine_of)

    for pair in range(2):
        for stream in range(4):
            came(stream, 2, pair + 2 * (1 - stream % 2))

    arrived(wbuf.at[:, :, other], w3_recv)
    wf[...] = wbuf[...].astype(F32).reshape(1024, 128)
    left = iota((128, 128), 1) < 64
    for h in range(8):
        part = wf[pl.ds(h, 128, stride=8), :]
        turned = pltpu.roll(part, 64, 1)
        w4[h * 128 : h * 128 + 128, 0:128] = jnp.where(left, part, turned).astype(BF16)
        w4[h * 128 : h * 128 + 128, 128:256] = jnp.where(left, turned, part).astype(BF16)

    def product0(d):
        zt = rot(z, d)
        part0[zt] = dot(g0[zt].reshape(128, 512), w4[0:512]).reshape(8, 16, 256)

    def product1(d):
        yt = rot(y, d)
        part1[yt] = dot(g1[:, yt].reshape(128, 512), w4[512:1024]).reshape(8, 16, 256)

    for d in (0, 1, 2, 3, 5, 6, 7):
        product0(d)
        product1(d)
    row = iota((128, ROWS), 0)
    owner = (row % 64) * 2 + row // 64
    mine = (own_v[...] == owner).astype(F32)
    earlier = (iota((ROWS, ROWS), 0) < iota((ROWS, ROWS), 1)).astype(F32).astype(BF16)
    before = dot(mine.astype(BF16), earlier)
    mine = mine * fin_v[...].astype(F32)
    for i in range(N):
        oh[i] = jnp.where(before == F32(i), mine, F32(0)).astype(BF16)
    a, b = iota((128, 128), 0), iota((128, 128), 1)
    source = (a // 4 % 2) * 64 + (a // 8 % 4) * 16 + (a // 32) * 4 + a % 4
    order = (b == source).astype(F32).astype(BF16)

    for pair in range(2):
        for stream in range(4):
            came(stream, 3, pair + 2 * (stream % 2))
    product0(4)
    product1(4)

    left8 = iota((8, 8, 128), 2) < 64
    own8 = iota((8, 8, 128), 1) // 4 == c
    for i in range(N):
        block = part0[i] + part1[:, i]
        block = block[:, 0:8] + block[:, 8:16]
        block = jnp.where(left8, block[:, :, 0:128], block[:, :, 128:256])
        block = jnp.where(own8, block + pltpu.roll(block, 4, 1), F32(0))
        pn[i * 64 : i * 64 + 64, :] = block.reshape(64, 128).astype(BF16)

    half = iota((64, 128), 1) < 64
    for d in (4, 3, 5, 2, 6, 1, 7, 0):
        xt = rot(x, d)
        chosen = dot(oh[xt], pn[...])
        first, second = chosen[0:64], chosen[64:128]
        ts[0, xt] = jnp.where(half, first, pltpu.roll(second, 64, 1)).astype(BF16)
        ts[1, xt] = jnp.where(half, pltpu.roll(first, 64, 1), second).astype(BF16)
        if d:
            remote(ts.at[0, xt], tr.at[x * 2 + c], t_send, t_recv, x=xt, c=0)
            remote(ts.at[1, xt], tr.at[x * 2 + c], t_send, t_recv, x=xt, c=1)
        else:
            remote(ts.at[other, x], tr.at[x * 2 + c], t_send, t_recv, c=other)
            tr[x * 2 + c] = ts[c, x]

    arrived(bg.at[pl.ds(0, 7)], b_recv)
    for i in range(N):
        block = bg[i].astype(F32)
        sgu[i * 64 : i * 64 + 32, :] = block.astype(BF16)
        sgu[i * 64 + 32 : i * 64 + 64, :] = pltpu.roll(block, 64, 1).astype(BF16)
    chosen = dot(oh[x], sgu[...])
    total = jnp.where(half, chosen[0:64], pltpu.roll(chosen[64:128], 64, 1))

    arrived(tr.at[pl.ds(0, 15)], t_recv)
    summed = tr[0].astype(F32)
    for i in range(1, 2 * N):
        summed = summed + tr[i].astype(F32)
    o1[...] = (total + summed).reshape(8, 8, 128).astype(BF16)

    def z_step(d, carry):
        zt = rot(z, d)
        remote(o1.at[zt], r1.at[z], z_send, z_recv, z=zt)
        return carry

    lax.fori_loop(1, N, z_step, 0)
    r1[z] = o1[z]

    for d in (4, 3, 5, 2, 6, 1, 7, 0):
        xt = rot(x, d)
        part = (part0[xt] + part1[:, xt]).reshape(128, 256)
        top, bottom = part[0:64], part[64:128]
        cs[0, xt] = jnp.where(half, top[:, 0:128], bottom[:, 0:128]).astype(BF16)
        cs[1, xt] = jnp.where(half, top[:, 128:256], bottom[:, 128:256]).astype(BF16)
        if d:
            remote(cs.at[0, xt], cr.at[x * 2 + c], c_send, c_recv, x=xt, c=0)
            remote(cs.at[1, xt], cr.at[x * 2 + c], c_send, c_recv, x=xt, c=1)
        else:
            remote(cs.at[other, x], cr.at[x * 2 + c], c_send, c_recv, c=other)
            cr[x * 2 + c] = cs[c, x]

    arrived(r1.at[pl.ds(0, 7)], z_recv)
    tf[...] = r1[...].astype(F32).reshape(64, 128)
    for i in range(N):
        t2[i] = tf[pl.ds(i, 8, stride=8), :].astype(BF16)

    def y_step(d, carry):
        yt = rot(y, d)
        remote(t2.at[yt], r2.at[y * 2 + c], y_send, y_recv, y=yt, c=0)
        remote(t2.at[yt], r2.at[y * 2 + c], y_send, y_recv, y=yt, c=1)
        return carry

    remote(t2.at[y], r2.at[y * 2 + c], y_send, y_recv, c=other)
    lax.fori_loop(1, N, y_step, 0)
    r2[y * 2 + c] = t2[y]

    arrived(cr.at[pl.ds(0, 15)], c_recv)
    summed = cr[pl.ds(0, 2)].astype(F32)
    for i in range(1, N):
        summed = summed + cr[pl.ds(2 * i, 2)].astype(F32)
    rows_out[...] = dot(order, summed.reshape(128, 128).astype(BF16)).astype(BF16)

    arrived(r2.at[pl.ds(0, 15)], y_recv)

    arrived(g0.at[pl.ds(0, 7), pl.ds(0, 2)], w_send.at[0])
    arrived(wbuf.at[:, :, c], w_send.at[1])
    arrived(g0.at[0, pl.ds(0, 7)], p_send.at[0])
    arrived(g0.at[0, pl.ds(0, 7)], p_send.at[1])
    for i in range(4):
        arrived(g0.at[pl.ds(0, 7), pl.ds(0, 4)], ring_send.at[i])
    arrived(cr.at[pl.ds(0, 15)], c_send)
    arrived(bg.at[pl.ds(0, 7)], b_send)
    arrived(tr.at[pl.ds(0, 15)], t_send)
    arrived(r1.at[pl.ds(0, 7)], z_send)
    arrived(r2.at[pl.ds(0, 15)], y_send)


def finish(rows_ref, r2_ref, upd_ref, tr_ref, tf):
    c = lax.axis_index(CA)
    rows = rows_ref[...].astype(F32)
    turned = pltpu.roll(rows, 64, 1)
    for t in range(4):
        upd_ref[t, 0:32, :] = rows[t * 32 : t * 32 + 32, 0:64].astype(BF16)
        upd_ref[t, 32:64, :] = turned[t * 32 : t * 32 + 32, 0:64].astype(BF16)
    eighth = iota((8, 128), 1) < 64
    for i in range(N):
        v0, v1 = r2_ref[2 * i].astype(F32), r2_ref[2 * i + 1].astype(F32)
        a0 = jnp.where(c == 0, v0, pltpu.roll(v0, 64, 1))
        a1 = jnp.where(c == 0, pltpu.roll(v1, 64, 1), v1)
        tf[i * 8 : i * 8 + 8, :] = jnp.where(eighth, a0, a1)
    for i in range(N):
        block = tf[pl.ds(i, 8, stride=8), :]
        for k in range(N):
            at = (i * N + k) * 128
            tr_ref[0, :, at : at + 128] = block[k : k + 1].astype(BF16)


def shards(base_stream, out_weight, queries, cache_keys, cache_values, new_keys, new_values, lengths, finished, owners):
    hbm = pl.BlockSpec(memory_space=pltpu.HBM)
    vmem = pl.BlockSpec(memory_space=pltpu.VMEM)
    dma = pltpu.SemaphoreType.DMA
    rows, handed = pl.pallas_call(
        kernel,
        out_shape=(jax.ShapeDtypeStruct((128, 128), BF16), jax.ShapeDtypeStruct((16, 8, 128), BF16)),
        in_specs=[hbm] * 10,
        out_specs=(vmem, vmem),
        scratch_shapes=[
            pltpu.SMEM((4,), I32),
            pltpu.VMEM((4, 4, 8, 128), BF16),
            pltpu.VMEM((4, FULL, 128), BF16),
            pltpu.VMEM((4, FULL, 128), BF16),
            pltpu.VMEM((16, 128), BF16),
            pltpu.VMEM((16, 128), BF16),
            pltpu.VMEM((64, 64), BF16),
            pltpu.VMEM((1, ROWS), I32),
            pltpu.VMEM((1, ROWS), I32),
            pltpu.VMEM((8, 4, 8, 128), BF16),
            pltpu.VMEM((8, 4, 8, 128), BF16),
            pltpu.VMEM((8, 8, 2, 8, 128), BF16),
            pltpu.VMEM((1024, 128), F32),
            pltpu.VMEM((1024, 256), BF16),
            pltpu.VMEM((128, 128), F32),
            pltpu.VMEM((8, 8, 16, 512), BF16),
            pltpu.VMEM((8, 8, 16, 512), BF16),
            pltpu.VMEM((8, 8, 16, 256), F32),
            pltpu.VMEM((8, 8, 16, 256), F32),
            pltpu.VMEM((ROWS, 128), BF16),
            pltpu.VMEM((2, 8, 64, 128), BF16),
            pltpu.VMEM((16, 64, 128), BF16),
            pltpu.VMEM((2, 8, 64, 128), BF16),
            pltpu.VMEM((16, 64, 128), BF16),
            pltpu.VMEM((32, 128), BF16),
            pltpu.VMEM((8, 32, 128), BF16),
            pltpu.VMEM((ROWS, 128), BF16),
            pltpu.VMEM((8, 128, ROWS), BF16),
            pltpu.VMEM((8, 8, 128), BF16),
            pltpu.VMEM((8, 8, 128), BF16),
            pltpu.VMEM((64, 128), F32),
            pltpu.VMEM((8, 8, 128), BF16),
            dma((10,)),
            dma((2, 4)),
            dma((2,)),
            dma,
            dma,
            dma,
            dma((2,)),
            dma((2, 4)),
            dma((4,)),
            dma((4, 14)),
            dma,
            dma,
            dma,
            dma,
            dma,
            dma,
            dma,
            dma,
            dma,
            dma,
        ],
        compiler_params=pltpu.CompilerParams(collective_id=0, has_side_effects=True, vmem_limit_bytes=24 << 20),
        name="decode",
    )(*(pltpu.with_memory_space_constraint(a, pltpu.HBM) for a in (
        lengths,
        queries,
        cache_keys.reshape(4, CTX, 128),
        cache_values.reshape(4, CTX, 128),
        new_keys.reshape(16, 128),
        new_values.reshape(16, 128),
        out_weight.reshape(8, 64, 128).transpose(1, 0, 2).reshape(4, 2, 4, 2, 8, 128),
        base_stream,
        owners.reshape(1, ROWS),
        finished.reshape(1, ROWS),
    )))
    return pl.pallas_call(
        finish,
        out_shape=(jax.ShapeDtypeStruct((4, 64, 64), BF16), jax.ShapeDtypeStruct((1, 1, 8192), BF16)),
        in_specs=[vmem, vmem],
        out_specs=(vmem, vmem),
        scratch_shapes=[pltpu.VMEM((64, 128), F32)],
        compiler_params=pltpu.CompilerParams(vmem_limit_bytes=4 << 20),
        name="finish",
    )(rows, handed)


def solution(mesh):
    torus = Mesh(mesh.devices.reshape(N, N, 2, N), (ZA, YA, CA, XA))
    placed = (
        P(XA, REPLICA),
        P(XA, REPLICA, None),
        P(None, REPLICA, XA, None),
        P(REPLICA, XA, None, None),
        P(REPLICA, XA, None, None),
        P(None, REPLICA, XA, None),
        P(None, REPLICA, XA, None),
        P(REPLICA),
        P(),
        P(),
    )
    return jax.shard_map(
        shards, mesh=torus, in_specs=placed, out_specs=(P(None, XA, REPLICA), P(REPLICA, XA, None)), check_vma=False
    )
```

```python
import functools
import math

import jax
import jax.numpy as jnp
from jax import lax
from jax.experimental import pallas as pl
from jax.experimental.pallas import tpu as pltpu
from jax.sharding import Mesh
from jax.sharding import PartitionSpec as P

ZA, YA, CA, XA = "replica_0", "replica_1", "replica_2", "tensor"
REPLICA = (ZA, YA, CA)
MESH = pl.DeviceIdType.MESH
F32, BF16, I32 = jnp.float32, jnp.bfloat16, jnp.int32
N = 8
CTX = 1536
PAD = 128
FULL = CTX + PAD
ROWS = 512
FAR_FIRST = (4, 3, 5, 2, 6, 1, 7, 0)


def dot(a, b):
    return jnp.dot(a, b, preferred_element_type=F32)


def iota(shape, dim):
    return lax.broadcasted_iota(I32, shape, dim)


def offset_of(j):
    return (j + 1) // 2 * (2 * (j % 2) - 1)


def mirror(j):
    if j == 0 or j == N - 1:
        return j
    return j + 1 if j % 2 else j - 1


def kernel(
    len_hbm, q_hbm, k_hbm, v_hbm, nk_hbm, nv_hbm, w_hbm, base_hbm, own_hbm, fin_hbm,
    rows_out, r2,
    len_s, q_v, k_v, v_v, nk_v, nv_v, base_v, own_v, fin_v,
    sa, sb, wbuf, wf, w4, att, g0, g1, part0, part1, vv, ps, pin, pn, ts, tr, cs, cr, oh, tf, t2,
    in_sem, kv_sem,
    w_send, w1_recv, w2_recv, w3_recv,
    p_send, p_recv, ring_send, ring_recv,
    known, u_send, u_recv, t_send, t_recv, c_send, c_recv, y_send, y_recv,
):
    z, y, c, x = (lax.axis_index(a) for a in (ZA, YA, CA, XA))
    other = 1 - c

    def rot(i, d):
        return lax.rem(i + d + N, N)

    def remote(src, dst, ssem, rsem, **to):
        pltpu.make_async_remote_copy(
            src_ref=src, dst_ref=dst, send_sem=ssem, recv_sem=rsem,
            device_id={{"z": ZA, "y": YA, "c": CA, "x": XA}[k]: v for k, v in to.items()},
            device_id_type=MESH,
        ).start()

    def arrived(ref, sem):
        pltpu.make_async_copy(ref, ref, sem).wait()

    small = [
        (q_hbm, q_v), (nk_hbm, nk_v), (nv_hbm, nv_v), (len_hbm, len_s),
        (base_hbm, base_v), (own_hbm, own_v), (fin_hbm, fin_v),
    ]
    loads = [pltpu.make_async_copy(a, b, in_sem.at[i]) for i, (a, b) in enumerate(small)]
    k_loads = [pltpu.make_async_copy(k_hbm.at[b], k_v.at[b, pl.ds(0, CTX)], kv_sem.at[0, b]) for b in range(4)]
    v_loads = [pltpu.make_async_copy(v_hbm.at[b], v_v.at[b, pl.ds(0, CTX)], kv_sem.at[1, b]) for b in range(4)]
    for load in loads[:4]:
        load.start()
    for b in range(4):
        k_loads[b].start()
        v_loads[b].start()
    for load in loads[4:]:
        load.start()

    barrier = pltpu.get_barrier_semaphore()

    def greet(**to):
        pl.semaphore_signal(
            barrier, inc=1, device_id={{"z": ZA, "y": YA, "c": CA, "x": XA}[k]: v for k, v in to.items()},
            device_id_type=MESH,
        )

    greet(c=other)

    def greet_step(d, carry):
        greet(z=rot(z, d))
        greet(y=rot(y, d), c=0)
        greet(y=rot(y, d), c=1)
        greet(x=rot(x, d), c=0)
        greet(x=rot(x, d), c=1)
        return carry

    lax.fori_loop(1, N, greet_step, 0)

    for load in loads[:4]:
        load.wait()
    nk, nv = nk_v[...], nv_v[...]
    for b in range(4):
        pick = (iota((PAD, 16), 1) == iota((PAD, 16), 0) * 4 + b).astype(F32).astype(BF16)
        k_v[b, CTX:FULL, :] = dot(pick, nk).astype(BF16)
        v_v[b, CTX:FULL, :] = dot(pick, nv).astype(BF16)

    scale = 1.0 / math.sqrt(128.0)

    def attend(b):
        q = q_v[:, b].astype(F32).reshape(32, 128).astype(BF16)
        scores = lax.dot_general(q, k_v[b], (((1,), (1,)), ((), ())), preferred_element_type=F32) * scale
        col = iota((32, FULL), 1)
        step = iota((32, FULL), 0) // 8
        keep = (col < len_s[b]) | ((col >= CTX) & (col - CTX <= step))
        scores = jnp.where(keep, scores, F32(-1e30))
        high = jnp.max(scores, axis=-1, keepdims=True)
        weight = jnp.exp(scores - high)
        total = jnp.sum(weight, axis=-1, keepdims=True)
        probs = (weight / total).astype(BF16)
        mixed = dot(probs, v_v[b])
        for t in range(4):
            att[pl.ds((t * 4 + b) * 8, 8), :] = mixed[t * 8 : t * 8 + 8]

    for first in (0, 2):
        for b in (first, first + 1):
            k_loads[b].wait()
            v_loads[b].wait()
        attend(first)
        attend(first + 1)
    for h in range(8):
        part = att[pl.ds(h, 16, stride=8), :].astype(BF16)
        (g0 if h < 4 else g1)[z, y, :, (h % 4) * 128 : (h % 4) * 128 + 128] = part
    pl.semaphore_wait(barrier, 5 * (N - 1) + 1)

    for j in range(1, N):
        o = offset_of(j)
        remote(g0.at[z, y], g0.at[z, y], p_send.at[0], p_recv.at[0, mirror(j) // 2], y=rot(y, o))
        remote(g1.at[z, y], g1.at[z, y], p_send.at[1], p_recv.at[1, mirror(j) // 2], z=rot(z, o))

    def unit(stream, s, j):
        o = offset_of(j)
        if stream == 0:
            return g0.at[rot(z, -s), rot(y, o)]
        if stream == 1:
            return g0.at[rot(z, s), rot(y, o)]
        if stream == 2:
            return g1.at[rot(z, o), rot(y, -s)]
        return g1.at[rot(z, o), rot(y, s)]

    def slot_of(s, pair):
        return s * 4 + (pair % 2 if isinstance(s, int) and s == 3 else pair)

    def forward(stream, s, pair, places=(0, 1)):
        to = ({"z": rot(z, 1)}, {"z": rot(z, -1)}, {"y": rot(y, 1)}, {"y": rot(y, -1)})[stream]
        for i in places:
            block = unit(stream, s, pair * 2 + i)
            remote(block, block, ring_send.at[stream], ring_recv.at[stream, slot_of(s, pair)], **to)

    def came(stream, s, pair):
        arrived(g0.at[0, pl.ds(0, 2)], ring_recv.at[stream, slot_of(s, pair)])

    for stream in range(4):
        forward(stream, 0, 0, (0,))

    def level0(pair):
        for half_of in range(2):
            arrived(g0.at[0, pl.ds(0, 2 if pair else 1)], p_recv.at[half_of, pair])
            for stream in (2 * half_of, 2 * half_of + 1):
                forward(stream, 0, pair, (0, 1) if pair else (1,))

    def via_z(zt):
        return w_hbm.at[zt // 2, zt % 2, :, zt % 2]

    def via_y(yt):
        return w_hbm.at[:, (yt + 1) % 2, yt // 2, yt % 2]

    own_w = [
        pltpu.make_async_copy(via_z(z), sa.at[z], in_sem.at[7]),
        pltpu.make_async_copy(via_y(y), sb.at[y], in_sem.at[8]),
    ]
    for load in own_w:
        load.start()

    def w1_step(d, carry):
        zt, yt = rot(z, d), rot(y, d)
        remote(via_z(zt), sa.at[z], w_send.at[0], w1_recv, z=zt)
        remote(via_y(yt), sb.at[y], w_send.at[0], w1_recv, y=yt)
        return carry

    lax.fori_loop(1, N, w1_step, 0)

    for pair in range(4):
        level0(pair)

    def known_step(d, carry):
        for core in range(2):
            pl.semaphore_signal(
                known, inc=1, device_id={XA: rot(x, d), CA: core}, device_id_type=MESH
            )
        return carry

    lax.fori_loop(1, N, known_step, 0)
    pl.semaphore_signal(known, inc=1, device_id={CA: other}, device_id_type=MESH)

    for load in own_w:
        load.wait()
    arrived(g0.at[0, pl.ds(0, 7)], w1_recv)
    even = (z + y) % 2 == 0

    def w2_step(i, carry):
        yt, zt = 2 * i + z % 2, 2 * i + (y + 1) % 2

        @pl.when(yt != y)
        def _():
            remote(sa.at[:, i], wbuf.at[:, y, c], w_send.at[0], w2_recv, y=yt)

        @pl.when(zt != z)
        def _():
            remote(sb.at[:, i], wbuf.at[z, :, c], w_send.at[0], w2_recv, z=zt)

        return carry

    lax.fori_loop(0, N // 2, w2_step, 0)

    @pl.when(even)
    def _():
        pltpu.make_async_copy(sa.at[:, y // 2], wbuf.at[:, y, c], in_sem.at[9]).start()

    @pl.when(jnp.logical_not(even))
    def _():
        pltpu.make_async_copy(sb.at[:, z // 2], wbuf.at[z, :, c], in_sem.at[9]).start()


    def ring_step(k, carry):
        s, pair = k // 4, k % 4
        for stream in range(4):
            at = (pair + s * (stream % 2)) % 4
            came(stream, s - 1, at)
            forward(stream, s, at)
        return carry

    lax.fori_loop(4, 12, ring_step, 0)

    arrived(g0.at[0, pl.ds(0, 1)], in_sem.at[9])
    arrived(g0.at[0, pl.ds(0, 7)], w2_recv)
    remote(wbuf.at[:, :, c], wbuf.at[:, :, c], w_send.at[1], w3_recv, c=other)

    for pair in range(2):
        for stream in range(4):
            mine_of = pair + 2 * (stream % 2)
            came(stream, 2, mine_of)
            forward(stream, 3, mine_of)

    for pair in range(2):
        for stream in range(4):
            came(stream, 2, pair + 2 * (1 - stream % 2))

    arrived(wbuf.at[:, :, other], w3_recv)
    wf[...] = wbuf[...].astype(F32).reshape(1024, 128)
    left = iota((128, 128), 1) < 64
    for h in range(8):
        part = wf[pl.ds(h, 128, stride=8), :]
        turned = pltpu.roll(part, 64, 1)
        w4[h * 128 : h * 128 + 128, 0:128] = jnp.where(left, part, turned).astype(BF16)
        w4[h * 128 : h * 128 + 128, 128:256] = jnp.where(left, turned, part).astype(BF16)

    def product0(d):
        zt = rot(z, d)
        part0[zt] = dot(g0[zt].reshape(128, 512), w4[0:512]).reshape(8, 16, 256)

    def product1(d):
        yt = rot(y, d)
        part1[yt] = dot(g1[:, yt].reshape(128, 512), w4[512:1024]).reshape(8, 16, 256)

    for d in (0, 1, 2, 3, 5, 6, 7):
        product0(d)
        product1(d)
    for load in loads[4:]:
        load.wait()
    row = iota((128, ROWS), 0)
    owner = (row % 64) * 2 + row // 64
    mine = (own_v[...] == owner).astype(F32)
    earlier = (iota((ROWS, ROWS), 0) < iota((ROWS, ROWS), 1)).astype(F32).astype(BF16)
    before = dot(mine.astype(BF16), earlier)
    mine = mine * fin_v[...].astype(F32)
    for i, d in enumerate(FAR_FIRST):
        oh[i] = jnp.where(before == rot(x, d).astype(F32), mine, F32(0)).astype(BF16)
    a, b = iota((128, 128), 0), iota((128, 128), 1)
    source = (a // 4 % 2) * 64 + (a // 8 % 4) * 16 + (a // 32) * 4 + a % 4
    order = (b == source).astype(F32).astype(BF16)

    for pair in range(2):
        for stream in range(4):
            came(stream, 3, pair + 2 * (stream % 2))
    product0(4)
    product1(4)

    base = base_v[...].astype(F32)
    base = jnp.where(iota((64, 128), 1) // 64 == c, jnp.concatenate([base, base], axis=1), F32(0))
    left8 = iota((8, 8, 128), 2) < 64
    own8 = iota((8, 8, 128), 1) // 4 == c
    low4 = iota((4, 8, 128), 1) < 4
    for i in range(N):
        block = part0[i] + part1[:, i]
        block = block[:, 0:8] + block[:, 8:16]
        block = jnp.where(left8, block[:, :, 0:128], block[:, :, 128:256])
        block = block + pltpu.roll(block, 4, 1)
        vv[i] = block
        block = block.reshape(4, 2, 8, 128)
        ps[i] = jnp.where(low4, block[:, 0], block[:, 1]).astype(BF16)
        if i % 4 == 3:
            group = pl.ds(i - 3, 4)
            remote(ps.at[group], pin.at[group], u_send, u_recv.at[i // 4], c=other)
    pl.semaphore_wait(known, 2 * N - 1)
    for i in range(N):
        if i % 4 == 0:
            arrived(pin.at[pl.ds(i, 4)], u_recv.at[i // 4])
        theirs = pin[i].astype(F32)
        turned = pltpu.roll(theirs, 4, 1)
        theirs = jnp.stack([jnp.where(low4, theirs, turned), jnp.where(low4, turned, theirs)], axis=1)
        block = jnp.where(own8, vv[i], theirs.reshape(8, 8, 128)).reshape(64, 128)
        pn[i * 64 : i * 64 + 64, :] = (block + jnp.where(x == i, base, F32(0))).astype(BF16)

    half = iota((64, 128), 1) < 64
    here = x * N + z
    for i in range(0, N, 2):
        chosen = dot(oh[i : i + 2].reshape(256, ROWS), pn[...])
        for k in range(2):
            first, second = chosen[k * 128 : k * 128 + 64], chosen[k * 128 + 64 : k * 128 + 128]
            to0 = jnp.where(half, first, pltpu.roll(second, 64, 1))
            to1 = jnp.where(half, pltpu.roll(first, 64, 1), second)
            ts[i + k] = jnp.where(c == 0, to0, to1).reshape(8, 8, 128).astype(BF16)
            d = FAR_FIRST[i + k]

            def t_step(j, carry, i=i, k=k, d=d):
                zt = rot(z, offset_of(N - 1 - j))
                remote(ts.at[i + k, zt], tr.at[here], t_send, t_recv, x=rot(x, d), z=zt)
                return carry

            lax.fori_loop(0, N if d else N - 1, t_step, 0)
    tr[here] = ts[N - 1, z]

    for d in FAR_FIRST:
        xt = rot(x, d)
        part = (part0[xt] + part1[:, xt]).reshape(128, 256)
        top, bottom = part[0:64], part[64:128]
        cs[0, xt] = jnp.where(half, top[:, 0:128], bottom[:, 0:128]).astype(BF16)
        cs[1, xt] = jnp.where(half, top[:, 128:256], bottom[:, 128:256]).astype(BF16)
        if d:
            remote(cs.at[0, xt], cr.at[x * 2 + c], c_send, c_recv, x=xt, c=0)
            remote(cs.at[1, xt], cr.at[x * 2 + c], c_send, c_recv, x=xt, c=1)
        else:
            remote(cs.at[other, x], cr.at[x * 2 + c], c_send, c_recv, c=other)
            cr[x * 2 + c] = cs[c, x]

    arrived(tr.at[pl.ds(0, 63)], t_recv)
    for i in range(N):
        block = tr[i].astype(F32)
        for k in range(1, N):
            block = block + tr[k * N + i].astype(F32)
        tf[i * 8 : i * 8 + 8, :] = block
    for i in range(N):
        t2[i] = tf[pl.ds(i, 8, stride=8), :].astype(BF16)

    def y_step(d, carry):
        yt = rot(y, d)
        remote(t2.at[yt], r2.at[y * 2 + c], y_send, y_recv, y=yt, c=0)
        remote(t2.at[yt], r2.at[y * 2 + c], y_send, y_recv, y=yt, c=1)
        return carry

    remote(t2.at[y], r2.at[y * 2 + c], y_send, y_recv, c=other)
    lax.fori_loop(1, N, y_step, 0)
    r2[y * 2 + c] = t2[y]

    arrived(cr.at[pl.ds(0, 15)], c_recv)
    summed = cr[pl.ds(0, 2)].astype(F32)
    for i in range(1, N):
        summed = summed + cr[pl.ds(2 * i, 2)].astype(F32)
    rows_out[...] = dot(order, summed.reshape(128, 128).astype(BF16)).astype(BF16)

    arrived(r2.at[pl.ds(0, 15)], y_recv)

    arrived(g0.at[pl.ds(0, 7), pl.ds(0, 2)], w_send.at[0])
    arrived(wbuf.at[:, :, c], w_send.at[1])
    arrived(g0.at[0, pl.ds(0, 7)], p_send.at[0])
    arrived(g0.at[0, pl.ds(0, 7)], p_send.at[1])
    for i in range(4):
        arrived(g0.at[pl.ds(0, 7), pl.ds(0, 4)], ring_send.at[i])
    arrived(cr.at[pl.ds(0, 15)], c_send)
    arrived(tr.at[pl.ds(0, 63)], t_send)
    arrived(pin, u_send)
    arrived(r2.at[pl.ds(0, 15)], y_send)


def finish(rows_ref, r2_ref, upd_ref, tr_ref, tf):
    c = lax.axis_index(CA)
    rows = rows_ref[...].astype(F32)
    turned = pltpu.roll(rows, 64, 1)
    for t in range(4):
        upd_ref[t, 0:32, :] = rows[t * 32 : t * 32 + 32, 0:64].astype(BF16)
        upd_ref[t, 32:64, :] = turned[t * 32 : t * 32 + 32, 0:64].astype(BF16)
    eighth = iota((8, 128), 1) < 64
    for i in range(N):
        v0, v1 = r2_ref[2 * i].astype(F32), r2_ref[2 * i + 1].astype(F32)
        a0 = jnp.where(c == 0, v0, pltpu.roll(v0, 64, 1))
        a1 = jnp.where(c == 0, pltpu.roll(v1, 64, 1), v1)
        tf[i * 8 : i * 8 + 8, :] = jnp.where(eighth, a0, a1)
    for i in range(N):
        block = tf[pl.ds(i, 8, stride=8), :]
        for k in range(N):
            at = (i * N + k) * 128
            tr_ref[0, :, at : at + 128] = block[k : k + 1].astype(BF16)


def shards(base_stream, out_weight, queries, cache_keys, cache_values, new_keys, new_values, lengths, finished, owners):
    hbm = pl.BlockSpec(memory_space=pltpu.HBM)
    vmem = pl.BlockSpec(memory_space=pltpu.VMEM)
    dma = pltpu.SemaphoreType.DMA
    rows, handed = pl.pallas_call(
        kernel,
        out_shape=(jax.ShapeDtypeStruct((128, 128), BF16), jax.ShapeDtypeStruct((16, 8, 128), BF16)),
        in_specs=[hbm] * 10,
        out_specs=(vmem, vmem),
        scratch_shapes=[
            pltpu.SMEM((4,), I32),
            pltpu.VMEM((4, 4, 8, 128), BF16),
            pltpu.VMEM((4, FULL, 128), BF16),
            pltpu.VMEM((4, FULL, 128), BF16),
            pltpu.VMEM((16, 128), BF16),
            pltpu.VMEM((16, 128), BF16),
            pltpu.VMEM((64, 64), BF16),
            pltpu.VMEM((1, ROWS), I32),
            pltpu.VMEM((1, ROWS), I32),
            pltpu.VMEM((8, 4, 8, 128), BF16),
            pltpu.VMEM((8, 4, 8, 128), BF16),
            pltpu.VMEM((8, 8, 2, 8, 128), BF16),
            pltpu.VMEM((1024, 128), F32),
            pltpu.VMEM((1024, 256), BF16),
            pltpu.VMEM((128, 128), F32),
            pltpu.VMEM((8, 8, 16, 512), BF16),
            pltpu.VMEM((8, 8, 16, 512), BF16),
            pltpu.VMEM((8, 8, 16, 256), F32),
            pltpu.VMEM((8, 8, 16, 256), F32),
            pltpu.VMEM((8, 8, 8, 128), F32),
            pltpu.VMEM((8, 4, 8, 128), BF16),
            pltpu.VMEM((8, 4, 8, 128), BF16),
            pltpu.VMEM((ROWS, 128), BF16),
            pltpu.VMEM((8, 8, 8, 128), BF16),
            pltpu.VMEM((64, 8, 128), BF16),
            pltpu.VMEM((2, 8, 64, 128), BF16),
            pltpu.VMEM((16, 64, 128), BF16),
            pltpu.VMEM((8, 128, ROWS), BF16),
            pltpu.VMEM((64, 128), F32),
            pltpu.VMEM((8, 8, 128), BF16),
            dma((10,)),
            dma((2, 4)),
            dma((2,)),
            dma,
            dma,
            dma,
            dma((2,)),
            dma((2, 4)),
            dma((4,)),
            dma((4, 14)),
            pltpu.SemaphoreType.REGULAR,
            dma,
            dma((2,)),
            dma,
            dma,
            dma,
            dma,
            dma,
            dma,
        ],
        compiler_params=pltpu.CompilerParams(collective_id=0, has_side_effects=True, vmem_limit_bytes=24 << 20),
        name="decode",
    )(*(pltpu.with_memory_space_constraint(a, pltpu.HBM) for a in (
        lengths,
        queries,
        cache_keys.reshape(4, CTX, 128),
        cache_values.reshape(4, CTX, 128),
        new_keys.reshape(16, 128),
        new_values.reshape(16, 128),
        out_weight.reshape(8, 64, 128).transpose(1, 0, 2).reshape(4, 2, 4, 2, 8, 128),
        base_stream,
        owners.reshape(1, ROWS),
        finished.reshape(1, ROWS),
    )))
    return pl.pallas_call(
        finish,
        out_shape=(jax.ShapeDtypeStruct((4, 64, 64), BF16), jax.ShapeDtypeStruct((1, 1, 8192), BF16)),
        in_specs=[vmem, vmem],
        out_specs=(vmem, vmem),
        scratch_shapes=[pltpu.VMEM((64, 128), F32)],
        compiler_params=pltpu.CompilerParams(vmem_limit_bytes=4 << 20),
        name="finish",
    )(rows, handed)


def solution(mesh):
    torus = Mesh(mesh.devices.reshape(N, N, 2, N), (ZA, YA, CA, XA))
    placed = (
        P(XA, REPLICA),
        P(XA, REPLICA, None),
        P(None, REPLICA, XA, None),
        P(REPLICA, XA, None, None),
        P(REPLICA, XA, None, None),
        P(None, REPLICA, XA, None),
        P(None, REPLICA, XA, None),
        P(REPLICA),
        P(),
        P(),
    )
    return jax.shard_map(
        shards, mesh=torus, in_specs=placed, out_specs=(P(None, XA, REPLICA), P(REPLICA, XA, None)), check_vma=False
    )
```
